32 devices in a mesh: groups: 2 (over y), inner: 4 (over z), outer: 4 (over x, core).
Axes of the slice: x: 2, y: 2, z: 4, core: 2. Of those that a mesh axis runs over, the one named last changes fastest.
Arguments:
- queries: bfloat16 [8192, 1024], P(('groups', 'outer', 'inner')), parts along dimension 0, may hold values from -6 to 6
- keys: bfloat16 [8192, 1024], P(('groups', 'outer', 'inner')), parts along dimension 0, may hold values from -6 to 6
- values: bfloat16 [8192, 1024], P(('groups', 'outer', 'inner')), parts along dimension 0, may hold values from -6 to 6
- retain: float32 [8192, 8], P(('groups', 'outer', 'inner')), parts along dimension 0, may hold values from 0.4 to 1
- step: float32 [8192, 8], P(('groups', 'outer', 'inner')), parts along dimension 0, may hold values from 0.000625 to 0.0125
- momentum: float32 [8192, 8], P(('groups', 'outer', 'inner')), parts along dimension 0, may hold values from 0.97 to 0.99
- init_memory: float32 [8, 128, 128], replicated, may hold values from -0.1875 to 0.1875
- init_momentum: float32 [8, 128, 128], replicated, may hold values from -0.1875 to 0.1875
Outputs:
- retrieved: bfloat16 [8192, 1024], P(('groups', 'outer', 'inner')), parts along dimension 0
The draws below stay inside these ranges and needn't reach their ends.
There are 2 independent parts, one for each index of `groups`. The reference program is written for one: setup_inputs(seed, part) draws one part's arguments, and reference() takes and returns one part's arrays. A program takes and returns all parts, laid end to end along the dimension named above; an argument that names none is the same for every part. Nothing has to cross between parts.
All inputs are finite; a program needn't handle non-finite values.
Results may differ from the reference program's by a relative error of at most 0.001.
Values sent between devices are 32-bit elements; how exact they have to be, the bound alone decides.
No kernel may reach another device: no remote copies, remote signals or barrier semaphores. Data moves between devices by JAX's collectives and lax.ppermute only.
A program may use at most 256 MiB of HBM per device.

```python
import math
import jax
import jax.numpy as jnp
from jax import lax

H = 8
DK = 128
BLOCK = 256
TOKENS = 4096
N_INNER = 4
N_OUTER = 4


def draw_retain(key, part):
    split_keys = jax.random.split(key, 4)
    lowest, highest = (0.2 / TOKENS, 1.0 / 40.0)
    rates = jnp.exp(jax.random.uniform(split_keys[0], (H,), jnp.float32, math.log(lowest), math.log(highest)))
    jitter = jax.random.uniform(split_keys[1], (TOKENS, H), jnp.float32, 0.5, 2.0)
    kept = jnp.exp(-rates[None, :] * jitter)
    spots = jax.random.randint(split_keys[2], (6,), 0, TOKENS)
    struck = jnp.any(jnp.arange(TOKENS)[:, None] == spots[None, :], axis=1)
    losses = jax.random.uniform(split_keys[3], (TOKENS, H), jnp.float32, 0.5, 0.8)
    return jnp.where(struck[:, None], kept * losses, kept).astype(jnp.float32)


def block_scale(key, shape, cuts, smallest, largest):
    factor_of, own = 1.0, jax.random.fold_in(key, 6)
    for dim, parts in cuts:
        draws = jnp.exp(jax.random.uniform(jax.random.fold_in(own, dim), (parts,), jnp.float32, smallest / len(cuts), largest / len(cuts)))
        factor_of = factor_of * jnp.repeat(draws, shape[dim] // parts).reshape([-1 if axis == dim else 1 for axis in range(len(shape))])
    return factor_of


def scatter_about(key, extent, deviation, bound, shards=(), kind=jnp.bfloat16):
    values = jax.random.normal(key, extent, jnp.float32) * deviation
    if len(shards) > 0:
        values = block_scale(key, extent, shards, -0.22, 0.18) * values
    return jnp.clip(values, min=-bound, max=bound).astype(kind)


def setup_inputs(seed: int = 0, part: int = 0) -> dict:
    splits = jax.random.split(jax.random.key(seed), 9)
    own_keys = jax.random.split(jax.random.fold_in(splits[8], part), 9)
    return {
        "queries": scatter_about(own_keys[0], (TOKENS, H * DK), 1.0, 6.0, ((0, 16),)),
        "keys": scatter_about(own_keys[1], (TOKENS, H * DK), 1.0, 6.0, ((0, 16),)),
        "values": scatter_about(own_keys[2], (TOKENS, H * DK), 1.0, 6.0, ((0, 16),)),
        "retain": draw_retain(jax.random.fold_in(jax.random.fold_in(splits[8], part), 71), part),
        "step": jnp.clip(jnp.exp(math.log(0.0125) - 2.9957323 * jax.random.uniform(own_keys[4], (TOKENS, H), jnp.float32) ** block_scale(own_keys[4], (TOKENS, H), ((0, 16),), -0.2, 0.2)), 0.000625, 0.0125),
        "momentum": jnp.clip(0.97 + 0.01999998 * jax.random.uniform(own_keys[5], (TOKENS, H), jnp.float32) ** block_scale(own_keys[5], (TOKENS, H), ((0, 16),), -0.2, 0.2), 0.97, 0.99),
        "init_memory": scatter_about(splits[6], (H, DK, DK), (8 * DK) ** -0.5, 0.1875, (), jnp.float32),
        "init_momentum": scatter_about(splits[7], (H, DK, DK), (8 * DK) ** -0.5, 0.1875, (), jnp.float32),
    }


def unit_rows(source, heads):
    rows = source.astype(jnp.float32).reshape(source.shape[0], heads, -1)
    return rows * lax.rsqrt(lax.optimization_barrier(jnp.sum(rows * rows, -1, keepdims=True)) + 1e-06)

def block_terms(queries, keys, values, retain, step, momentum):
    length = queries.shape[0]
    heads = retain.shape[1]
    precise = lax.Precision.HIGHEST
    query_unit = unit_rows(queries, heads)
    key_unit = unit_rows(keys, heads)
    value_rows = values.astype(jnp.float32).reshape(length, heads, -1)
    key_width = key_unit.shape[2]
    log_retain = jnp.cumsum(jnp.log(retain), 0).T
    log_moment = jnp.cumsum(jnp.log(momentum), 0).T
    position = jnp.arange(length)
    causal = (position[:, None] >= position[None, :])[None]
    retain_decay = jnp.where(causal, jnp.exp(jnp.where(causal, log_retain[:, :, None] - log_retain[:, None, :], 0.0)), 0.0)
    momentum_decay = jnp.where(causal, jnp.exp(jnp.where(causal, log_moment[:, :, None] - log_moment[:, None, :], 0.0)), 0.0)
    weights = jnp.einsum('htu,hur->htr', retain_decay, momentum_decay, precision=precise)
    carry_scale = jnp.einsum('htu,hu->ht', retain_decay, jnp.exp(log_moment), precision=precise)
    scores = jnp.einsum('thd,rhd->htr', query_unit, key_unit, precision=precise)
    step_rows = step.T
    mixing = scores * weights * step_rows[:, None, :]
    memory_weight = weights[:, -1, :] * step_rows
    moment_weight = jnp.exp(log_moment[:, -1:] - log_moment) * step_rows
    memory_gram = jnp.einsum('rhd,hr,rhe->hde', key_unit, memory_weight, key_unit, precision=precise)
    moment_gram = jnp.einsum('rhd,hr,rhe->hde', key_unit, moment_weight, key_unit, precision=precise)
    identity = jnp.eye(key_width, dtype=jnp.float32)[None]
    retain_end = jnp.exp(log_retain[:, -1])[:, None, None]
    moment_end = jnp.exp(log_moment[:, -1])[:, None, None]
    carry_end = carry_scale[:, -1][:, None, None]
    upper_rows = jnp.concatenate([retain_end * identity - memory_gram, -moment_gram], axis=2)
    lower_rows = jnp.concatenate([carry_end * identity, moment_end * identity], axis=2)
    transition = jnp.concatenate([upper_rows, lower_rows], axis=1)
    memory_write = jnp.einsum('rhd,hr,rhe->hde', value_rows, memory_weight, key_unit, precision=precise)
    moment_write = jnp.einsum('rhd,hr,rhe->hde', value_rows, moment_weight, key_unit, precision=precise)
    offset = jnp.concatenate([memory_write, moment_write], axis=2)
    local_terms = (query_unit, key_unit, value_rows, jnp.exp(log_retain), carry_scale, mixing)
    return (transition, offset, local_terms)

def block_output(carried, local_terms):
    query_unit, key_unit, value_rows, retain_scale, carry_scale, mixing = local_terms
    precise = lax.Precision.HIGHEST
    key_width = query_unit.shape[2]
    memory = carried[:, :, :key_width]
    moment_part = carried[:, :, key_width:]
    residual = jnp.einsum('rhd,hed->hre', key_unit, memory, precision=precise) - jnp.transpose(value_rows, (1, 0, 2))
    result = retain_scale[:, :, None] * jnp.einsum('thd,hed->hte', query_unit, memory, precision=precise)
    result = result + carry_scale[:, :, None] * jnp.einsum('thd,hed->hte', query_unit, moment_part, precision=precise)
    result = result - jnp.einsum('htr,hre->hte', mixing, residual, precision=precise)
    return jnp.transpose(result, (1, 0, 2)).reshape(query_unit.shape[0], -1).astype(jnp.bfloat16)

def advance_state(carried, transition, offset):
    return jnp.einsum('hij,hjk->hik', carried, transition, precision=lax.Precision.HIGHEST) + offset

def reference(queries, keys, values, retain, step, momentum, init_memory, init_momentum):
    blocks = N_INNER * N_OUTER
    first_state = jnp.concatenate([init_memory, init_momentum], axis=2)

    def one_block(carried, pieces):
        transition, offset, local_terms = block_terms(*pieces)
        result = block_output(carried, local_terms)
        return (advance_state(carried, transition, offset), result)
    pieces = (queries.reshape(blocks, BLOCK, -1), keys.reshape(blocks, BLOCK, -1), values.reshape(blocks, BLOCK, -1), retain.reshape(blocks, BLOCK, -1), step.reshape(blocks, BLOCK, -1), momentum.reshape(blocks, BLOCK, -1))
    final_state, results = lax.scan(one_block, first_state, pieces)
    return results.reshape(TOKENS, -1)
```

```python
import functools

import jax
import jax.numpy as jnp
from jax import lax
from jax.experimental import pallas as pl
from jax.experimental.pallas import tpu as pltpu
from jax.sharding import PartitionSpec as P

TAIL = 8
EPS = 1e-06
EXACT = lax.Precision.HIGHEST


def halves(x):
    high = x.astype(jnp.bfloat16)
    return high, (x - high.astype(jnp.float32)).astype(jnp.bfloat16)


def mul(a, b, dims):
    return lax.dot_general(a, b, (dims, ((), ())), preferred_element_type=jnp.float32)


def mul_tn(a, b):
    return mul(a, b, ((0,), (0,)))


def mul_nt(a, b):
    return mul(a, b, ((1,), (1,)))


def mul_nn(a, b):
    return mul(a, b, ((1,), (0,)))


def grid_ids(shape):
    return lax.broadcasted_iota(jnp.int32, shape, 0), lax.broadcasted_iota(jnp.int32, shape, 1)


def running_logs(retain, momentum):
    length = retain.shape[0]
    row, col = grid_ids((length, length))
    lower = (row >= col).astype(jnp.float32)
    log_retain = jnp.dot(lower, jnp.log(retain), precision=EXACT, preferred_element_type=jnp.float32)
    log_moment = jnp.dot(lower, jnp.log(momentum), precision=EXACT, preferred_element_type=jnp.float32)
    return log_retain, log_moment


def map_kernel(heads, width, k_ref, v_ref, retain_ref, step_ref, momentum_ref, out_ref):
    length = k_ref.shape[0]
    step = step_ref[...]
    log_retain, log_moment = running_logs(retain_ref[...], momentum_ref[...])
    row, col = grid_ids((length, length))
    upper = (row <= col).astype(jnp.float32)
    decay = jnp.exp(log_moment)
    reach = jnp.exp(log_retain[length - 1 :, :] - log_retain) * decay
    suffix = jnp.dot(upper, reach, precision=EXACT, preferred_element_type=jnp.float32)
    memory_weight = suffix / decay * step
    moment_weight = jnp.exp(log_moment[length - 1 :, :] - log_moment) * step
    retain_end = jnp.exp(log_retain[length - 1 :, :])
    moment_end = decay[length - 1 :, :]
    carry_end = suffix[:1, :]
    drow, dcol = grid_ids((width, width))
    keep = drow <= dcol
    diagonal = drow == dcol
    for h in range(heads):
        lanes = slice(h * width, (h + 1) * width)
        keys = k_ref[:, lanes]
        values = v_ref[:, lanes]
        wide = keys.astype(jnp.float32)
        scale = lax.rsqrt(jnp.sum(wide * wide, -1, keepdims=True) + EPS)
        weight_m = memory_weight[:, h : h + 1] * scale
        weight_s = moment_weight[:, h : h + 1] * scale
        write = jnp.concatenate([wide * weight_m, wide * weight_s], axis=1)
        high, low = halves(write)
        offset = mul_tn(values, high) + mul_tn(values, low)
        high, low = halves(write * scale)
        gram = mul_tn(keys, high) + mul_tn(keys, low)
        moment_gram = gram[:, width:]
        out_ref[h, :width, :] = jnp.where(keep, gram[:, :width], moment_gram)
        out_ref[h, width : 2 * width, :] = offset[:, :width]
        out_ref[h, 2 * width : 3 * width, :] = offset[:, width:]
        on_diagonal = jnp.sum(jnp.where(diagonal, moment_gram, 0.0), axis=0, keepdims=True)
        wide_row = lambda x: jnp.broadcast_to(x[:, h : h + 1], (1, width))
        out_ref[h, 3 * width :, :] = jnp.concatenate(
            [
                on_diagonal,
                wide_row(retain_end),
                wide_row(moment_end),
                wide_row(carry_end),
                jnp.zeros((TAIL - 4, width), jnp.float32),
            ],
            axis=0,
        )


def read_kernel(
    heads, width, q_ref, k_ref, v_ref, retain_ref, step_ref, momentum_ref, high_ref, low_ref, base_ref
):
    length = k_ref.shape[0]
    log_retain, log_moment = running_logs(retain_ref[...], momentum_ref[...])
    row, col = grid_ids((length, length))
    causal = row >= col
    lower = causal.astype(jnp.bfloat16)
    identity = (row == col).astype(jnp.float32)
    flip = lambda x: lax.dot_general(
        x, identity, (((0,), (0,)), ((), ())), precision=EXACT, preferred_element_type=jnp.float32
    )
    log_gap = flip(log_moment - log_retain)
    step_rows = flip(step_ref[...] * jnp.exp(-log_moment))
    retain_scale = jnp.exp(log_retain)
    ones = jnp.ones((8, width), jnp.bfloat16)
    for h in range(heads):
        lanes = slice(h * width, (h + 1) * width)
        queries, keys, values = q_ref[:, lanes], k_ref[:, lanes], v_ref[:, lanes]
        wide_q = queries.astype(jnp.float32)
        wide_k = keys.astype(jnp.float32)
        query_scale = lax.rsqrt(jnp.sum(wide_q * wide_q, -1, keepdims=True) + EPS)
        high, low = halves(wide_k * wide_k)
        key_scale = lax.rsqrt((mul_nt(ones, high) + mul_nt(ones, low))[:1, :] + EPS)
        gap = log_retain[:, h : h + 1] + log_gap[h : h + 1, :]
        reach = jnp.exp(jnp.where(causal, gap, -1e30))
        high, low = halves(reach)
        weights = mul_nn(high, lower) + mul_nn(low, lower)
        mixing = mul_nt(queries, keys) * weights * (step_rows[h : h + 1, :] * key_scale)
        high, low = halves(mixing)
        base_ref[h] = query_scale * (mul_nn(high, values) + mul_nn(low, values))
        high, low = halves(mixing * key_scale)
        seen = mul_nn(high, keys) + mul_nn(low, keys)
        unit_q = query_scale * wide_q
        reads = jnp.concatenate(
            [retain_scale[:, h : h + 1] * unit_q - query_scale * seen, weights[:, :1] * unit_q], axis=1
        )
        high, low = halves(reads)
        high_ref[h] = high
        low_ref[h] = low


def scan_kernel(width, keep_states, merged, flag_ref, maps_ref, entry_ref, *refs):
    if merged:
        other_ref, *refs = refs
        entry = jnp.where(flag_ref[0] > 0, other_ref[...], entry_ref[...])
    else:
        entry = entry_ref[...]
    blocks = maps_ref.shape[0]
    row, col = grid_ids((width, width))
    if not keep_states and merged:
        refs[1][...] = entry
    state = entry
    for b in range(blocks):
        if keep_states:
            refs[0][b] = state
            if b == blocks - 1:
                return
        packed = maps_ref[b, :width, :]
        flipped = packed.T
        tail = maps_ref[b, 3 * width :, :]
        gram = jnp.concatenate(
            [
                jnp.where(row <= col, packed, flipped),
                jnp.where(row == col, tail[:1, :], jnp.where(row > col, packed, flipped)),
            ],
            axis=1,
        )
        gram_high, gram_low = halves(gram)
        memory, moment = state[:, :width], state[:, width:]
        high, low = halves(memory)
        seen = mul_nn(high, gram_high) + (mul_nn(high, gram_low) + mul_nn(low, gram_high))
        new_memory = (
            tail[1:2, :] * memory + tail[3:4, :] * moment + maps_ref[b, width : 2 * width, :] - seen[:, :width]
        )
        new_moment = tail[2:3, :] * moment + maps_ref[b, 2 * width : 3 * width, :] - seen[:, width:]
        state = jnp.concatenate([new_memory, new_moment], axis=1)
    refs[0][...] = state


def output_kernel(heads, width, states_ref, high_ref, low_ref, base_ref, out_ref):
    for h in range(heads):
        high, low = halves(states_ref[h])
        read_high = high_ref[h]
        result = base_ref[h] + mul_nt(read_high, high)
        result = result + (mul_nt(read_high, low) + mul_nt(low_ref[h], high))
        out_ref[:, h * width : (h + 1) * width] = result.astype(out_ref.dtype)


def whole(n):
    return [pl.BlockSpec(memory_space=pltpu.VMEM)] * n


def f32(*shape):
    return jax.ShapeDtypeStruct(shape, jnp.float32)


LIMIT = pltpu.CompilerParams(vmem_limit_bytes=48 << 20)


def local(n_outer, n_inner, queries, keys, values, retain, step, momentum, init_memory, init_moment):
    length, heads = retain.shape
    width = init_memory.shape[2]
    axes = ("inner", "outer")
    place = lambda f: (f % n_inner) * n_outer + f // n_inner
    sections = n_outer * n_inner // heads
    teams = [[place(s * heads + j) for j in range(heads)] for s in range(sections)]
    position = lax.axis_index("outer") * n_inner + lax.axis_index("inner")
    section, mine = position // heads, position % heads

    maps = pl.pallas_call(
        functools.partial(map_kernel, heads, width),
        out_shape=f32(heads, 3 * width + TAIL, width),
        in_specs=whole(5),
        out_specs=pl.BlockSpec(memory_space=pltpu.VMEM),
        compiler_params=LIMIT,
    )(keys, values, retain, step, momentum)
    maps = lax.all_to_all(maps, axes, 0, 0, axis_index_groups=teams, tiled=True)

    read_high, read_low, base = pl.pallas_call(
        functools.partial(read_kernel, heads, width),
        out_shape=(
            jax.ShapeDtypeStruct((heads, length, 2 * width), jnp.bfloat16),
            jax.ShapeDtypeStruct((heads, length, 2 * width), jnp.bfloat16),
            f32(heads, length, width),
        ),
        in_specs=whole(6),
        out_specs=tuple(whole(3)),
        compiler_params=LIMIT,
    )(queries, keys, values, retain, step, momentum)

    entry = jnp.concatenate(
        [
            lax.dynamic_index_in_dim(init_memory, mine, 0, keepdims=False),
            lax.dynamic_index_in_dim(init_moment, mine, 0, keepdims=False),
        ],
        axis=1,
    )

    def scan(flag, entry, other, keep_states):
        merged = other is not None
        state = f32(width, 2 * width)
        out = f32(heads, width, 2 * width) if keep_states else (state, state) if merged else state
        given = (entry, other) if merged else (entry,)
        return pl.pallas_call(
            functools.partial(scan_kernel, width, keep_states, merged),
            out_shape=out,
            in_specs=[pl.BlockSpec(memory_space=pltpu.SMEM)] + whole(1 + len(given)),
            out_specs=jax.tree.map(lambda _: pl.BlockSpec(memory_space=pltpu.VMEM), out),
            compiler_params=LIMIT,
        )(flag.astype(jnp.int32).reshape(1), maps, *given)

    other, flag = None, section
    for s in range(sections - 1):
        if s == 0:
            final = scan(flag, entry, None, False)
        else:
            final, entry = scan(flag, entry, other, False)
        other = lax.ppermute(final, axes, list(zip(teams[s], teams[s + 1])))
        flag = section == s + 1
    states = scan(flag, entry, other, True)
    states = lax.all_to_all(states, axes, 0, 0, axis_index_groups=teams, tiled=True)

    return pl.pallas_call(
        functools.partial(output_kernel, heads, width),
        out_shape=jax.ShapeDtypeStruct((length, heads * width), jnp.bfloat16),
        in_specs=whole(4),
        out_specs=pl.BlockSpec(memory_space=pltpu.VMEM),
        compiler_params=LIMIT,
    )(states, read_high, read_low, base)


def solution(mesh):
    rows = P(("groups", "outer", "inner"), None)
    return jax.shard_map(
        functools.partial(local, mesh.shape["outer"], mesh.shape["inner"]),
        mesh=mesh,
        in_specs=(rows,) * 6 + (P(), P()),
        out_specs=rows,
        check_vma=False,
    )
```

```python
import functools

import jax
import jax.numpy as jnp
from jax import lax
from jax.experimental import pallas as pl
from jax.experimental.pallas import tpu as pltpu
from jax.sharding import PartitionSpec as P

CHUNKS = 1
TAIL = 8
EPS = 1e-06
EXACT = lax.Precision.HIGHEST


def halves(x):
    high = x.astype(jnp.bfloat16)
    return high, (x - high.astype(jnp.float32)).astype(jnp.bfloat16)


def mul(a, b, dims):
    return lax.dot_general(a, b, (dims, ((), ())), preferred_element_type=jnp.float32)


def mul_tn(a, b):
    return mul(a, b, ((0,), (0,)))


def mul_nt(a, b):
    return mul(a, b, ((1,), (1,)))


def mul_nn(a, b):
    return mul(a, b, ((1,), (0,)))


def exact(a, b):
    return jnp.dot(a, b, precision=EXACT, preferred_element_type=jnp.float32)


def grid_ids(shape):
    return lax.broadcasted_iota(jnp.int32, shape, 0), lax.broadcasted_iota(jnp.int32, shape, 1)


def fetch(sources, targets, sem):
    copies = [
        pltpu.make_async_copy(s, t, sem.at[n]) for n, (s, t) in enumerate(zip(sources, targets))
    ]
    for copy in copies:
        copy.start()
    return copies


def map_kernel(heads, width, chunks, mine_ref, *refs):
    hbm = refs[:5]
    outs = refs[5 : 5 + chunks * heads]
    k_ref, v_ref, retain_ref, step_ref, momentum_ref, *made, in_sem = refs[5 + chunks * heads :]
    rows = width // chunks
    copies = fetch(hbm, (k_ref, v_ref, retain_ref, step_ref, momentum_ref), in_sem)
    length = k_ref.shape[0]
    row, col = grid_ids((length, length))
    before = (row <= col).astype(jnp.float32)
    after = (row >= col).astype(jnp.float32)
    drow, dcol = grid_ids((width, width))
    keep = drow <= dcol
    diagonal = drow == dcol
    for copy in copies[2:]:
        copy.wait()
    step = step_ref[...]
    logs = exact(jnp.concatenate([jnp.log(retain_ref[...]), jnp.log(momentum_ref[...])], axis=0), before)
    log_retain, log_moment = logs[:heads], logs[heads:]
    decay = jnp.exp(log_moment)
    reach = jnp.exp(log_retain[:, length - 1 :] - log_retain) * decay
    suffix = exact(reach, after)
    memory_weight = (suffix / decay * step).T
    moment_weight = (jnp.exp(log_moment[:, length - 1 :] - log_moment) * step).T
    retain_end = jnp.exp(log_retain[:, length - 1 :])
    moment_end = decay[:, length - 1 :]
    carry_end = suffix[:, :1]
    for copy in copies[:2]:
        copy.wait()
    for h in range(heads):
        lanes = slice(h * width, (h + 1) * width)
        keys = k_ref[:, lanes]
        values = v_ref[:, lanes]
        wide = keys.astype(jnp.float32)
        scale = lax.rsqrt(jnp.sum(wide * wide, -1, keepdims=True) + EPS)
        weight_m = memory_weight[:, h : h + 1] * scale
        weight_s = moment_weight[:, h : h + 1] * scale
        write = jnp.concatenate([wide * weight_m, wide * weight_s], axis=1)
        high, low = halves(write)
        offset = mul_tn(values, high) + mul_tn(values, low)
        high, low = halves(write * scale)
        gram = mul_tn(keys, high) + mul_tn(keys, low)
        moment_gram = gram[:, width:]
        on_diagonal = jnp.sum(jnp.where(diagonal, moment_gram, 0.0), axis=0, keepdims=True)
        wide_row = lambda x: jnp.broadcast_to(x[h : h + 1, :], (1, width))
        made[0][h, :width, :] = jnp.where(keep, gram[:, :width], moment_gram)
        made[0][h, width : width + TAIL, :] = jnp.concatenate(
            [
                on_diagonal,
                wide_row(retain_end),
                wide_row(moment_end),
                wide_row(carry_end),
                jnp.zeros((TAIL - 4, width), jnp.float32),
            ],
            axis=0,
        )
        for c in range(chunks):
            at = width + TAIL if c == 0 else 0
            part = offset[c * rows : (c + 1) * rows]
            made[c][h, at : at + rows, :] = part[:, :width]
            made[c][h, at + rows : at + 2 * rows, :] = part[:, width:]
    mine = mine_ref[0]
    for c in range(chunks):
        for s in range(heads):
            outs[c * heads + s][...] = made[c][lax.rem(mine + s, heads)]


def read_kernel(
    heads, width, q_ref, k_ref, v_ref, retain_ref, step_ref, momentum_ref, high_ref, low_ref, base_ref
):
    length = k_ref.shape[0]
    row, col = grid_ids((length, length))
    before = (row <= col).astype(jnp.float32)
    causal = row >= col
    lower = causal.astype(jnp.bfloat16)
    logs = exact(jnp.concatenate([jnp.log(retain_ref[...]), jnp.log(momentum_ref[...])], axis=0), before)
    log_retain, log_moment = logs[:heads], logs[heads:]
    log_gap = log_moment - log_retain
    step_rows = step_ref[...] * jnp.exp(-log_moment)
    log_column = log_retain.T
    retain_scale = jnp.exp(log_column)
    ones = jnp.ones((8, width), jnp.bfloat16)
    for h in range(heads):
        lanes = slice(h * width, (h + 1) * width)
        queries, keys, values = q_ref[:, lanes], k_ref[:, lanes], v_ref[:, lanes]
        wide_q = queries.astype(jnp.float32)
        wide_k = keys.astype(jnp.float32)
        query_scale = lax.rsqrt(jnp.sum(wide_q * wide_q, -1, keepdims=True) + EPS)
        high, low = halves(wide_k * wide_k)
        key_scale = lax.rsqrt((mul_nt(ones, high) + mul_nt(ones, low))[:1, :] + EPS)
        gap = log_column[:, h : h + 1] + log_gap[h : h + 1, :]
        reach = jnp.exp(jnp.where(causal, gap, -1e30))
        high, low = halves(reach)
        weights = mul_nn(high, lower) + mul_nn(low, lower)
        mixing = mul_nt(queries, keys) * weights * (step_rows[h : h + 1, :] * key_scale)
        high, low = halves(mixing)
        base_ref[h] = query_scale * (mul_nn(high, values) + mul_nn(low, values))
        high, low = halves(mixing * key_scale)
        seen = mul_nn(high, keys) + mul_nn(low, keys)
        unit_q = query_scale * wide_q
        reads = jnp.concatenate(
            [retain_scale[:, h : h + 1] * unit_q - query_scale * seen, weights[:, :1] * unit_q], axis=1
        )
        high, low = halves(reads)
        high_ref[h] = high
        low_ref[h] = low


def scan_kernel(heads, width, chunk, chunks, keep_states, merged, scalar_ref, entry_ref, *refs):
    rows = width // chunks
    here = slice(chunk * rows, (chunk + 1) * rows) if entry_ref.shape[0] == width else slice(0, rows)
    entry = entry_ref[here]
    if merged:
        other_ref, *refs = refs
        entry = jnp.where(scalar_ref[1] > 0, other_ref[...], entry)
    given = heads if chunk == 0 else 2 * heads
    arrived, refs = refs[:given], refs[given:]
    outs, refs = (refs[:heads], refs[heads:]) if keep_states else (refs[: 1 + merged], refs[1 + merged :])
    first_ref = refs[0]
    offset_ref = refs[1] if chunk > 0 else first_ref
    mine = scalar_ref[0]
    for n, ref in enumerate(arrived):
        target = first_ref if n < heads else offset_ref
        target[lax.rem(mine + heads - n % heads, heads)] = ref[...]
    row, col = grid_ids((width, width))
    at = 0 if chunk > 0 else width + TAIL
    if not keep_states and merged:
        outs[1][...] = entry
    if keep_states:
        states_ref = refs[-1]
    state = entry
    for b in range(heads):
        if keep_states:
            states_ref[b] = state
            if b == heads - 1:
                break
        packed = first_ref[b, :width, :]
        flipped = packed.T
        tail = first_ref[b, width : width + TAIL, :]
        gram = jnp.concatenate(
            [
                jnp.where(row <= col, packed, flipped),
                jnp.where(row == col, tail[:1, :], jnp.where(row > col, packed, flipped)),
            ],
            axis=1,
        )
        gram_high, gram_low = halves(gram)
        memory, moment = state[:, :width], state[:, width:]
        high, low = halves(memory)
        seen = mul_nn(high, gram_high) + (mul_nn(high, gram_low) + mul_nn(low, gram_high))
        new_memory = (
            tail[1:2, :] * memory + tail[3:4, :] * moment + offset_ref[b, at : at + rows, :] - seen[:, :width]
        )
        new_moment = tail[2:3, :] * moment + offset_ref[b, at + rows : at + 2 * rows, :] - seen[:, width:]
        state = jnp.concatenate([new_memory, new_moment], axis=1)
    if not keep_states:
        outs[0][...] = state
        return
    for s in range(heads):
        outs[s][...] = states_ref[lax.rem(mine + s, heads)]


def output_kernel(heads, width, chunks, mine_ref, *refs):
    arrived, refs = refs[: heads * chunks], refs[heads * chunks :]
    read_high_ref, read_low_ref, base_ref, out_ref = refs
    mine = mine_ref[0]
    for s in range(heads):
        h = lax.rem(mine + heads - s, heads)
        high, low = halves(jnp.concatenate([arrived[c * heads + s][...] for c in range(chunks)], axis=0))
        read_high = read_high_ref[h]
        result = base_ref[h] + mul_nt(read_high, high)
        result = result + (mul_nt(read_high, low) + mul_nt(read_low_ref[h], high))
        lanes = pl.ds(pl.multiple_of(h * width, width), width)
        out_ref[:, lanes] = result.astype(out_ref.dtype)


VMEM = pl.BlockSpec(memory_space=pltpu.VMEM)
HBM = pl.BlockSpec(memory_space=pltpu.HBM)
SMEM = pl.BlockSpec(memory_space=pltpu.SMEM)
LIMIT = pltpu.CompilerParams(vmem_limit_bytes=24 << 20)
DMA = pltpu.SemaphoreType.DMA


def f32(*shape):
    return jax.ShapeDtypeStruct(shape, jnp.float32)


def local(n_outer, n_inner, queries, keys, values, retain, step, momentum, init_memory, init_moment):
    length, heads = retain.shape
    width = init_memory.shape[2]
    chunks = CHUNKS
    rows = width // chunks
    axes = ("inner", "outer")
    place = lambda f: (f % n_inner) * n_outer + f // n_inner
    sections = n_outer * n_inner // heads
    teams = [[place(s * heads + j) for j in range(heads)] for s in range(sections)]
    position = lax.axis_index("outer") * n_inner + lax.axis_index("inner")
    section, mine = position // heads, position % heads
    scalars = lambda *xs: jnp.stack([jnp.asarray(x).astype(jnp.int32) for x in xs])
    gates = (retain.T, step.T, momentum.T)

    def swap(pieces):
        moved = [pieces[0]]
        for s in range(1, heads):
            pairs = [(team[j], team[(j + s) % heads]) for team in teams for j in range(heads)]
            moved.append(lax.ppermute(pieces[s], axes, pairs))
        return moved

    shapes = [(width + TAIL + 2 * rows, width)] + [(2 * rows, width)] * (chunks - 1)
    made = pl.pallas_call(
        functools.partial(map_kernel, heads, width, chunks),
        out_shape=[f32(*shape) for shape in shapes for _ in range(heads)],
        in_specs=[SMEM] + [HBM] * 5,
        out_specs=[VMEM] * (chunks * heads),
        scratch_shapes=[pltpu.VMEM(keys.shape, keys.dtype)] * 2
        + [pltpu.VMEM((heads, length), jnp.float32)] * 3
        + [pltpu.VMEM((heads, *shape), jnp.float32) for shape in shapes]
        + [DMA((5,))],
        compiler_params=LIMIT,
    )(scalars(mine), keys, values, *gates)
    maps = [swap(made[c * heads : (c + 1) * heads]) for c in range(chunks)]

    read_high, read_low, base = pl.pallas_call(
        functools.partial(read_kernel, heads, width),
        out_shape=(
            jax.ShapeDtypeStruct((heads, length, 2 * width), jnp.bfloat16),
            jax.ShapeDtypeStruct((heads, length, 2 * width), jnp.bfloat16),
            f32(heads, length, width),
        ),
        in_specs=[VMEM] * 6,
        out_specs=(VMEM,) * 3,
        compiler_params=LIMIT,
    )(queries, keys, values, *gates)

    start = jnp.concatenate(
        [
            lax.dynamic_index_in_dim(init_memory, mine, 0, keepdims=False),
            lax.dynamic_index_in_dim(init_moment, mine, 0, keepdims=False),
        ],
        axis=1,
    )

    def scan(c, flag, entry, other, keep_states):
        merged = other is not None
        state = f32(rows, 2 * width)
        out = [state] * (heads if keep_states else 1 + merged)
        given = ([other] if merged else []) + maps[0] + (maps[c] if c > 0 else [])
        scratch = [pltpu.VMEM((heads, *shapes[0]), jnp.float32)]
        if c > 0:
            scratch.append(pltpu.VMEM((heads, *shapes[c]), jnp.float32))
        if keep_states:
            scratch.append(pltpu.VMEM((heads, rows, 2 * width), jnp.float32))
        return pl.pallas_call(
            functools.partial(scan_kernel, heads, width, c, chunks, keep_states, merged),
            out_shape=out,
            in_specs=[SMEM, VMEM] + [VMEM] * len(given),
            out_specs=[VMEM] * len(out),
            scratch_shapes=scratch,
            compiler_params=LIMIT,
        )(scalars(mine, flag), entry, *given)

    states = []
    for c in range(chunks):
        entry, other, flag = start, None, section
        for s in range(sections - 1):
            final, *kept = scan(c, flag, entry, other, False)
            if kept:
                entry = kept[0]
            other = lax.ppermute(final, axes, list(zip(teams[s], teams[s + 1])))
            flag = section == s + 1
        states += swap(scan(c, flag, entry, other, True))

    return pl.pallas_call(
        functools.partial(output_kernel, heads, width, chunks),
        out_shape=jax.ShapeDtypeStruct((length, heads * width), jnp.bfloat16),
        in_specs=[SMEM] + [VMEM] * (heads * chunks + 3),
        out_specs=VMEM,
        compiler_params=LIMIT,
    )(scalars(mine), *states, read_high, read_low, base)


def solution(mesh):
    rows = P(("groups", "outer", "inner"), None)
    return jax.shard_map(
        functools.partial(local, mesh.shape["outer"], mesh.shape["inner"]),
        mesh=mesh,
        in_specs=(rows,) * 6 + (P(), P()),
        out_specs=rows,
        check_vma=False,
    )
```

```python
import functools

import jax
import jax.numpy as jnp
from jax import lax
from jax.experimental import pallas as pl
from jax.experimental.pallas import tpu as pltpu
from jax.sharding import PartitionSpec as P

FIRSTS = (1, 2, 3, 4, 5, 6, 7)
ORDER = (2, 4, 6, 3, 5, 1, 7)
READ = 1
HELD = 6
EARLY = 5
TAIL = 8
EPS = 1e-06
EXACT = lax.Precision.HIGHEST


def halves(x):
    high = x.astype(jnp.bfloat16)
    return high, (x - high.astype(jnp.float32)).astype(jnp.bfloat16)


def mul(a, b, dims):
    return lax.dot_general(a, b, (dims, ((), ())), preferred_element_type=jnp.float32)


def mul_tn(a, b):
    return mul(a, b, ((0,), (0,)))


def mul_nt(a, b):
    return mul(a, b, ((1,), (1,)))


def mul_nn(a, b):
    return mul(a, b, ((1,), (0,)))


def exact(a, b):
    return jnp.dot(a, b, precision=EXACT, preferred_element_type=jnp.float32)


def grid_ids(shape):
    return lax.broadcasted_iota(jnp.int32, shape, 0), lax.broadcasted_iota(jnp.int32, shape, 1)


def lanes_of(h, width):
    return pl.ds(pl.multiple_of(h * width, width), width)


def map_kernel(heads, width, shifts, mine_ref, *refs):
    hbm, outs = refs[:5], refs[5 : 5 + len(shifts)]
    *held, sem = refs[5 + len(shifts) :]
    k_ref, v_ref, retain_ref, step_ref, momentum_ref = held
    copies = [pltpu.make_async_copy(s, t, sem.at[n]) for n, (s, t) in enumerate(zip(hbm, held))]
    for copy in copies[2:] + copies[:2]:
        copy.start()
    mine = mine_ref[0]
    length = k_ref.shape[0]
    row, col = grid_ids((length, length))
    before = (row <= col).astype(jnp.float32)
    after = (row >= col).astype(jnp.float32)
    drow, dcol = grid_ids((width, width))
    keep = drow <= dcol
    diagonal = drow == dcol
    for copy in copies[2:]:
        copy.wait()
    from_mine = lambda ref: pltpu.roll(ref[...], lax.rem(heads - mine, heads), 0)
    step = from_mine(step_ref)
    logs = exact(
        jnp.concatenate([jnp.log(from_mine(retain_ref)), jnp.log(from_mine(momentum_ref))], axis=0), before
    )
    log_retain, log_moment = logs[:heads], logs[heads:]
    decay = jnp.exp(log_moment)
    reach = jnp.exp(log_retain[:, length - 1 :] - log_retain) * decay
    suffix = exact(reach, after)
    memory_weight = (suffix / decay * step).T
    moment_weight = (jnp.exp(log_moment[:, length - 1 :] - log_moment) * step).T
    retain_end = jnp.exp(log_retain[:, length - 1 :])
    moment_end = decay[:, length - 1 :]
    carry_end = suffix[:, :1]
    for copy in copies[:2]:
        copy.wait()
    for n, s in enumerate(shifts):
        lanes = lanes_of(lax.rem(mine + s, heads), width)
        keys = k_ref[:, lanes]
        values = v_ref[:, lanes]
        wide = keys.astype(jnp.float32)
        scale = lax.rsqrt(jnp.sum(wide * wide, -1, keepdims=True) + EPS)
        weight_m = memory_weight[:, s : s + 1] * scale
        weight_s = moment_weight[:, s : s + 1] * scale
        write = jnp.concatenate([wide * weight_m, wide * weight_s], axis=1)
        high, low = halves(write)
        offset = mul_tn(values, high) + mul_tn(values, low)
        high, low = halves(write * scale)
        gram = mul_tn(keys, high) + mul_tn(keys, low)
        moment_gram = gram[:, width:]
        on_diagonal = jnp.sum(jnp.where(diagonal, moment_gram, 0.0), axis=0, keepdims=True)
        wide_row = lambda x: jnp.broadcast_to(x[s : s + 1, :], (1, width))
        out = outs[n]
        out[:width, :] = jnp.where(keep, gram[:, :width], moment_gram)
        out[width : 2 * width, :] = offset[:, :width]
        out[2 * width : 3 * width, :] = offset[:, width:]
        out[3 * width :, :] = jnp.concatenate(
            [
                on_diagonal,
                wide_row(retain_end),
                wide_row(moment_end),
                wide_row(carry_end),
                jnp.zeros((TAIL - 4, width), jnp.float32),
            ],
            axis=0,
        )


def read_kernel(
    heads, width, q_ref, k_ref, v_ref, retain_ref, step_ref, momentum_ref, high_ref, low_ref, base_ref
):
    length = k_ref.shape[0]
    row, col = grid_ids((length, length))
    before = (row <= col).astype(jnp.float32)
    causal = row >= col
    lower = causal.astype(jnp.bfloat16)
    logs = exact(jnp.concatenate([jnp.log(retain_ref[...]), jnp.log(momentum_ref[...])], axis=0), before)
    log_retain, log_moment = logs[:heads], logs[heads:]
    log_gap = log_moment - log_retain
    step_rows = step_ref[...] * jnp.exp(-log_moment)
    log_column = log_retain.T
    retain_scale = jnp.exp(log_column)
    ones = jnp.ones((8, width), jnp.bfloat16)
    for h in range(heads):
        lanes = slice(h * width, (h + 1) * width)
        queries, keys, values = q_ref[:, lanes], k_ref[:, lanes], v_ref[:, lanes]
        wide_q = queries.astype(jnp.float32)
        wide_k = keys.astype(jnp.float32)
        query_scale = lax.rsqrt(jnp.sum(wide_q * wide_q, -1, keepdims=True) + EPS)
        high, low = halves(wide_k * wide_k)
        key_scale = lax.rsqrt((mul_nt(ones, high) + mul_nt(ones, low))[:1, :] + EPS)
        gap = log_column[:, h : h + 1] + log_gap[h : h + 1, :]
        reach = jnp.exp(jnp.where(causal, gap, -1e30))
        high, low = halves(reach)
        weights = mul_nn(high, lower) + mul_nn(low, lower)
        mixing = mul_nt(queries, keys) * weights * (step_rows[h : h + 1, :] * key_scale)
        high, low = halves(mixing)
        base_ref[h] = query_scale * (mul_nn(high, values) + mul_nn(low, values))
        high, low = halves(mixing * key_scale)
        seen = mul_nn(high, keys) + mul_nn(low, keys)
        unit_q = query_scale * wide_q
        reads = jnp.concatenate(
            [retain_scale[:, h : h + 1] * unit_q - query_scale * seen, weights[:, :1] * unit_q], axis=1
        )
        high, low = halves(reads)
        high_ref[h] = high
        low_ref[h] = low


def steps(width, state, high_ref, low_ref, offset_ref, count, keep=None):
    for b in range(count):
        if keep is not None:
            keep[b] = state
        tail = offset_ref[b, 2 * width :, :]
        memory, moment = state[:, :width], state[:, width:]
        high, low = halves(memory)
        seen = mul_nn(high, high_ref[b]) + (mul_nn(high, low_ref[b]) + mul_nn(low, high_ref[b]))
        new_memory = tail[1:2, :] * memory + tail[3:4, :] * moment + offset_ref[b, :width, :] - seen[:, :width]
        new_moment = tail[2:3, :] * moment + offset_ref[b, width : 2 * width, :] - seen[:, width:]
        state = jnp.concatenate([new_memory, new_moment], axis=1)
    return state


def unpack_kernel(heads, width, order, mine_ref, entry_ref, *refs):
    arrived, (high_ref, low_ref, offset_ref, final_ref) = refs[:heads], refs[heads:]
    mine = mine_ref[0]
    row, col = grid_ids((width, width))
    for n, s in enumerate(order):
        b = lax.rem(mine + heads - s, heads)
        packed = arrived[n][:width, :]
        flipped = packed.T
        diagonal = arrived[n][3 * width : 3 * width + 1, :]
        gram = jnp.concatenate(
            [
                jnp.where(row <= col, packed, flipped),
                jnp.where(row == col, diagonal, jnp.where(row > col, packed, flipped)),
            ],
            axis=1,
        )
        high, low = halves(gram)
        high_ref[b] = high
        low_ref[b] = low
        offset_ref[b] = arrived[n][width:, :]
    final_ref[...] = steps(width, entry_ref[...], high_ref, low_ref, offset_ref, heads)


def final_kernel(heads, width, flag_ref, entry_ref, other_ref, high_ref, low_ref, offset_ref, kept_ref, final_ref):
    entry = jnp.where(flag_ref[0] > 0, other_ref[...], entry_ref[...])
    kept_ref[...] = entry
    final_ref[...] = steps(width, entry, high_ref, low_ref, offset_ref, heads)


def states_kernel(heads, width, scalar_ref, entry_ref, other_ref, high_ref, low_ref, offset_ref, *refs):
    outs, keep = refs[:heads], refs[heads]
    mine = scalar_ref[1]
    entry = jnp.where(scalar_ref[0] > 0, other_ref[...], entry_ref[...])
    keep[heads - 1] = steps(width, entry, high_ref, low_ref, offset_ref, heads - 1, keep)
    for s in range(heads):
        outs[s][...] = keep[lax.rem(mine + s, heads)]


def read_out(h, state, read_high_ref, read_low_ref, base_ref):
    high, low = halves(state)
    read_high = read_high_ref[h]
    result = base_ref[h] + mul_nt(read_high, high)
    return (result + (mul_nt(read_high, low) + mul_nt(read_low_ref[h], high))).astype(jnp.bfloat16)


def early_kernel(heads, mine_ref, read_high_ref, read_low_ref, base_ref, *refs):
    *arrived, out_ref = refs
    mine = mine_ref[0]
    for s, ref in enumerate(arrived):
        h = lax.rem(mine + heads - s, heads)
        out_ref[s] = read_out(h, ref[...], read_high_ref, read_low_ref, base_ref)


def output_kernel(heads, width, mine_ref, read_high_ref, read_low_ref, base_ref, early_ref, *refs):
    *arrived, out_ref = refs
    mine = mine_ref[0]
    early = heads - len(arrived)
    for s in range(heads):
        h = lax.rem(mine + heads - s, heads)
        if s < early:
            result = early_ref[s]
        else:
            result = read_out(h, arrived[s - early][...], read_high_ref, read_low_ref, base_ref)
        out_ref[:, lanes_of(h, width)] = result


VMEM = pl.BlockSpec(memory_space=pltpu.VMEM)
HBM = pl.BlockSpec(memory_space=pltpu.HBM)
SMEM = pl.BlockSpec(memory_space=pltpu.SMEM)
LIMIT = pltpu.CompilerParams(vmem_limit_bytes=24 << 20)


def shape(kind, *sizes):
    return jax.ShapeDtypeStruct(sizes, kind)


def local(n_outer, n_inner, queries, keys, values, retain, step, momentum, init_memory, init_moment):
    length, heads = retain.shape
    width = init_memory.shape[2]
    f32, bf16 = jnp.float32, jnp.bfloat16
    axes = ("inner", "outer")
    place = lambda f: (f % n_inner) * n_outer + f // n_inner
    sections = n_outer * n_inner // heads
    teams = [[place(s * heads + j) for j in range(heads)] for s in range(sections)]
    position = lax.axis_index("outer") * n_inner + lax.axis_index("inner")
    section, mine = position // heads, position % heads
    scalars = lambda *xs: jnp.stack([jnp.asarray(x).astype(jnp.int32) for x in xs])
    gates = (retain.T, step.T, momentum.T)

    def call(kernel, out, given, spaces=VMEM, scratch=(), outs=VMEM):
        return pl.pallas_call(
            kernel,
            out_shape=out,
            in_specs=[SMEM] + [spaces] * (len(given) - 1),
            out_specs=jax.tree.map(lambda _: outs, out),
            scratch_shapes=scratch,
            compiler_params=LIMIT,
        )(*given)

    def shift(piece, s):
        pairs = [(team[j], team[(j + s) % heads]) for team in teams for j in range(heads)]
        return lax.ppermute(piece, axes, pairs)

    turns = [s for s in ORDER if s < heads]

    def swap(pieces):
        moved = {0: pieces[0], **{s: shift(pieces[s], s) for s in turns}}
        return [moved[s] for s in range(heads)]

    def behind(xs, y):
        return list(lax.optimization_barrier((*xs, y))[:-1])

    def make(shifts, given):
        given = [pltpu.with_memory_space_constraint(x, pltpu.HBM) for x in given]
        return call(
            functools.partial(map_kernel, heads, width, shifts),
            [shape(f32, 3 * width + TAIL, width)] * len(shifts),
            (scalars(mine), *given),
            HBM,
            [pltpu.VMEM(x.shape, x.dtype) for x in given] + [pltpu.SemaphoreType.DMA((len(given),))],
        )

    order = [*FIRSTS, 0]
    made = dict(zip(order, make(order, (keys, values, *gates))))
    maps = {0: made[0], **{s: shift(made[s], s) for s in order[:-1]}}
    maps = [maps[s] for s in order]

    start = jnp.concatenate(
        [
            lax.dynamic_index_in_dim(init_memory, mine, 0, keepdims=False),
            lax.dynamic_index_in_dim(init_moment, mine, 0, keepdims=False),
        ],
        axis=1,
    )
    state = shape(f32, width, 2 * width)
    *unpacked, final = call(
        functools.partial(unpack_kernel, heads, width, order),
        [
            shape(bf16, heads, width, 2 * width),
            shape(bf16, heads, width, 2 * width),
            shape(f32, heads, 2 * width + TAIL, width),
            state,
        ],
        (scalars(mine), start, *maps),
    )
    entry, other, flag = start, start, section < 0
    for s in range(sections - 1):
        if s > 0:
            entry, final = call(
                functools.partial(final_kernel, heads, width), [state] * 2, (scalars(flag), entry, other, *unpacked)
            )
        other = lax.ppermute(final, axes, list(zip(teams[s], teams[s + 1])))
        flag = section == s + 1
    states = call(
        functools.partial(states_kernel, heads, width),
        [state] * heads,
        (scalars(flag, mine), entry, other, *unpacked),
        scratch=[pltpu.VMEM((heads, width, 2 * width), f32)],
    )
    pieces, moved = states, {0: states[0]}
    for n, s in enumerate(turns):
        if n == READ:
            given = behind((queries, keys, values, *gates), moved[turns[0]])
            reads = pl.pallas_call(
                functools.partial(read_kernel, heads, width),
                out_shape=[
                    shape(bf16, heads, length, 2 * width),
                    shape(bf16, heads, length, 2 * width),
                    shape(f32, heads, length, width),
                ],
                in_specs=[VMEM] * 6,
                out_specs=[VMEM] * 3,
                compiler_params=LIMIT,
            )(*given,)
        piece = pieces[s] if n < HELD else behind([pieces[s]], reads[2])[0]
        moved[s] = shift(piece, s)
    states = [moved[s] for s in range(heads)]
    early = call(
        functools.partial(early_kernel, heads),
        shape(bf16, EARLY, length, width),
        (scalars(mine), *reads, *states[:EARLY]),
    )
    return call(
        functools.partial(output_kernel, heads, width),
        shape(bf16, length, heads * width),
        (scalars(mine), *reads, early, *states[EARLY:]),
    )


def solution(mesh):
    rows = P(("groups", "outer", "inner"), None)
    return jax.shard_map(
        functools.partial(local, mesh.shape["outer"], mesh.shape["inner"]),
        mesh=mesh,
        in_specs=(rows,) * 6 + (P(), P()),
        out_specs=rows,
        check_vma=False,
    )
```

```python
import functools

import jax
import jax.numpy as jnp
from jax import lax
from jax.experimental import pallas as pl
from jax.experimental.pallas import tpu as pltpu
from jax.sharding import PartitionSpec as P

FIRSTS = (1, 2, 3, 4, 5, 6, 7, 0)
ORDER = (2, 4, 6, 3, 5, 0, 1, 7)
READ = 1
HELD = 7
EARLY = 5
TAIL = 8
EPS = 1e-06
EXACT = lax.Precision.HIGHEST


def halves(x):
    high = x.astype(jnp.bfloat16)
    return high, (x - high.astype(jnp.float32)).astype(jnp.bfloat16)


def mul(a, b, dims):
    return lax.dot_general(a, b, (dims, ((), ())), preferred_element_type=jnp.float32)


def mul_tn(a, b):
    return mul(a, b, ((0,), (0,)))


def mul_nt(a, b):
    return mul(a, b, ((1,), (1,)))


def mul_nn(a, b):
    return mul(a, b, ((1,), (0,)))


def exact(a, b):
    return jnp.dot(a, b, precision=EXACT, preferred_element_type=jnp.float32)


def grid_ids(shape):
    return lax.broadcasted_iota(jnp.int32, shape, 0), lax.broadcasted_iota(jnp.int32, shape, 1)


def lanes_of(h, width):
    return pl.ds(pl.multiple_of(h * width, width), width)


def map_kernel(heads, width, shifts, mine_ref, *refs):
    hbm, outs = refs[:5], refs[5 : 5 + len(shifts)]
    *held, sem = refs[5 + len(shifts) :]
    k_ref, v_ref, retain_ref, step_ref, momentum_ref = held
    copies = [pltpu.make_async_copy(s, t, sem.at[n]) for n, (s, t) in enumerate(zip(hbm, held))]
    for copy in copies[2:] + copies[:2]:
        copy.start()
    mine = mine_ref[0]
    length = k_ref.shape[0]
    row, col = grid_ids((length, length))
    before = (row <= col).astype(jnp.float32)
    after = (row >= col).astype(jnp.float32)
    drow, dcol = grid_ids((width, width))
    keep = drow <= dcol
    diagonal = drow == dcol
    for copy in copies[2:]:
        copy.wait()
    from_mine = lambda ref: pltpu.roll(ref[...], lax.rem(heads - mine, heads), 0)
    step = from_mine(step_ref)
    logs = exact(
        jnp.concatenate([jnp.log(from_mine(retain_ref)), jnp.log(from_mine(momentum_ref))], axis=0), before
    )
    log_retain, log_moment = logs[:heads], logs[heads:]
    decay = jnp.exp(log_moment)
    reach = jnp.exp(log_retain[:, length - 1 :] - log_retain) * decay
    suffix = exact(reach, after)
    memory_weight = (suffix / decay * step).T
    moment_weight = (jnp.exp(log_moment[:, length - 1 :] - log_moment) * step).T
    retain_end = jnp.exp(log_retain[:, length - 1 :])
    moment_end = decay[:, length - 1 :]
    carry_end = suffix[:, :1]
    for copy in copies[:2]:
        copy.wait()
    for n, s in enumerate(shifts):
        lanes = lanes_of(lax.rem(mine + s, heads), width)
        keys = k_ref[:, lanes]
        values = v_ref[:, lanes]
        wide = keys.astype(jnp.float32)
        scale = lax.rsqrt(jnp.sum(wide * wide, -1, keepdims=True) + EPS)
        weight_m = memory_weight[:, s : s + 1] * scale
        weight_s = moment_weight[:, s : s + 1] * scale
        write = jnp.concatenate([wide * weight_m, wide * weight_s], axis=1)
        high, low = halves(write)
        offset = mul_tn(values, high) + mul_tn(values, low)
        high, low = halves(write * scale)
        gram = mul_tn(keys, high) + mul_tn(keys, low)
        moment_gram = gram[:, width:]
        on_diagonal = jnp.sum(jnp.where(diagonal, moment_gram, 0.0), axis=0, keepdims=True)
        wide_row = lambda x: jnp.broadcast_to(x[s : s + 1, :], (1, width))
        out = outs[n]
        out[:width, :] = jnp.where(keep, gram[:, :width], moment_gram)
        out[width : 2 * width, :] = offset[:, :width]
        out[2 * width : 3 * width, :] = offset[:, width:]
        out[3 * width :, :] = jnp.concatenate(
            [
                on_diagonal,
                wide_row(retain_end),
                wide_row(moment_end),
                wide_row(carry_end),
                jnp.zeros((TAIL - 4, width), jnp.float32),
            ],
            axis=0,
        )


def read_kernel(
    heads, width, q_ref, k_ref, v_ref, retain_ref, step_ref, momentum_ref, high_ref, low_ref, base_ref
):
    length = k_ref.shape[0]
    row, col = grid_ids((length, length))
    before = (row <= col).astype(jnp.float32)
    causal = row >= col
    lower = causal.astype(jnp.bfloat16)
    logs = exact(jnp.concatenate([jnp.log(retain_ref[...]), jnp.log(momentum_ref[...])], axis=0), before)
    log_retain, log_moment = logs[:heads], logs[heads:]
    log_gap = log_moment - log_retain
    step_rows = step_ref[...] * jnp.exp(-log_moment)
    log_column = log_retain.T
    retain_scale = jnp.exp(log_column)
    ones = jnp.ones((8, width), jnp.bfloat16)
    for h in range(heads):
        lanes = slice(h * width, (h + 1) * width)
        queries, keys, values = q_ref[:, lanes], k_ref[:, lanes], v_ref[:, lanes]
        wide_q = queries.astype(jnp.float32)
        wide_k = keys.astype(jnp.float32)
        query_scale = lax.rsqrt(jnp.sum(wide_q * wide_q, -1, keepdims=True) + EPS)
        high, low = halves(wide_k * wide_k)
        key_scale = lax.rsqrt((mul_nt(ones, high) + mul_nt(ones, low))[:1, :] + EPS)
        gap = log_column[:, h : h + 1] + log_gap[h : h + 1, :]
        reach = jnp.exp(jnp.where(causal, gap, -1e30))
        high, low = halves(reach)
        weights = mul_nn(high, lower) + mul_nn(low, lower)
        mixing = mul_nt(queries, keys) * weights * (step_rows[h : h + 1, :] * key_scale)
        high, low = halves(mixing)
        base_ref[h] = query_scale * (mul_nn(high, values) + mul_nn(low, values))
        high, low = halves(mixing * key_scale)
        seen = mul_nn(high, keys) + mul_nn(low, keys)
        unit_q = query_scale * wide_q
        reads = jnp.concatenate(
            [retain_scale[:, h : h + 1] * unit_q - query_scale * seen, weights[:, :1] * unit_q], axis=1
        )
        high, low = halves(reads)
        high_ref[h] = high
        low_ref[h] = low


def steps(width, state, high_ref, low_ref, offset_ref, count, keep=None):
    for b in range(count):
        if keep is not None:
            keep[b] = state
        tail = offset_ref[b, 2 * width :, :]
        memory, moment = state[:, :width], state[:, width:]
        high, low = halves(memory)
        seen = mul_nn(high, high_ref[b]) + (mul_nn(high, low_ref[b]) + mul_nn(low, high_ref[b]))
        new_memory = tail[1:2, :] * memory + tail[3:4, :] * moment + offset_ref[b, :width, :] - seen[:, :width]
        new_moment = tail[2:3, :] * moment + offset_ref[b, width : 2 * width, :] - seen[:, width:]
        state = jnp.concatenate([new_memory, new_moment], axis=1)
    return state


def unpack_kernel(heads, width, order, mine_ref, entry_ref, *refs):
    arrived, (high_ref, low_ref, offset_ref, final_ref) = refs[:heads], refs[heads:]
    mine = mine_ref[0]
    row, col = grid_ids((width, width))
    for n, s in enumerate(order):
        b = lax.rem(mine + heads - s, heads)
        packed = arrived[n][:width, :]
        flipped = packed.T
        diagonal = arrived[n][3 * width : 3 * width + 1, :]
        gram = jnp.concatenate(
            [
                jnp.where(row <= col, packed, flipped),
                jnp.where(row == col, diagonal, jnp.where(row > col, packed, flipped)),
            ],
            axis=1,
        )
        high, low = halves(gram)
        high_ref[b] = high
        low_ref[b] = low
        offset_ref[b] = arrived[n][width:, :]
    final_ref[...] = steps(width, entry_ref[...], high_ref, low_ref, offset_ref, heads)


def final_kernel(heads, width, flag_ref, entry_ref, other_ref, high_ref, low_ref, offset_ref, kept_ref, final_ref):
    entry = jnp.where(flag_ref[0] > 0, other_ref[...], entry_ref[...])
    kept_ref[...] = entry
    final_ref[...] = steps(width, entry, high_ref, low_ref, offset_ref, heads)


def states_kernel(heads, width, scalar_ref, entry_ref, other_ref, high_ref, low_ref, offset_ref, *refs):
    outs, keep = refs[:heads], refs[heads]
    mine = scalar_ref[1]
    entry = jnp.where(scalar_ref[0] > 0, other_ref[...], entry_ref[...])
    keep[heads - 1] = steps(width, entry, high_ref, low_ref, offset_ref, heads - 1, keep)
    for s in range(heads):
        outs[s][...] = keep[lax.rem(mine + s, heads)]


def read_out(h, state, read_high_ref, read_low_ref, base_ref):
    high, low = halves(state)
    read_high = read_high_ref[h]
    result = base_ref[h] + mul_nt(read_high, high)
    return (result + (mul_nt(read_high, low) + mul_nt(read_low_ref[h], high))).astype(jnp.bfloat16)


def early_kernel(heads, mine_ref, read_high_ref, read_low_ref, base_ref, *refs):
    *arrived, out_ref = refs
    mine = mine_ref[0]
    for s, ref in enumerate(arrived):
        h = lax.rem(mine + heads - s, heads)
        out_ref[s] = read_out(h, ref[...], read_high_ref, read_low_ref, base_ref)


def output_kernel(heads, width, mine_ref, read_high_ref, read_low_ref, base_ref, early_ref, *refs):
    *arrived, out_ref = refs
    mine = mine_ref[0]
    early = heads - len(arrived)
    for s in range(heads):
        h = lax.rem(mine + heads - s, heads)
        if s < early:
            result = early_ref[s]
        else:
            result = read_out(h, arrived[s - early][...], read_high_ref, read_low_ref, base_ref)
        out_ref[:, lanes_of(h, width)] = result


VMEM = pl.BlockSpec(memory_space=pltpu.VMEM)
HBM = pl.BlockSpec(memory_space=pltpu.HBM)
SMEM = pl.BlockSpec(memory_space=pltpu.SMEM)
LIMIT = pltpu.CompilerParams(vmem_limit_bytes=24 << 20)


def shape(kind, *sizes):
    return jax.ShapeDtypeStruct(sizes, kind)


def local(n_outer, n_inner, queries, keys, values, retain, step, momentum, init_memory, init_moment):
    length, heads = retain.shape
    width = init_memory.shape[2]
    f32, bf16 = jnp.float32, jnp.bfloat16
    axes = ("inner", "outer")
    place = lambda f: (f % n_inner) * n_outer + f // n_inner
    sections = n_outer * n_inner // heads
    teams = [[place(s * heads + j) for j in range(heads)] for s in range(sections)]
    position = lax.axis_index("outer") * n_inner + lax.axis_index("inner")
    mine = position % heads
    if heads % n_inner == 0 and n_outer == sections * (heads // n_inner):
        owners = [
            [place((h // n_inner * sections + s) * n_inner + h % n_inner) for h in range(heads)]
            for s in range(sections)
        ]
        outer = lax.axis_index("outer")
        section, head = outer % sections, outer // sections * n_inner + lax.axis_index("inner")
    else:
        owners, section, head = teams, position // heads, mine
    scalars = lambda *xs: jnp.stack([jnp.asarray(x).astype(jnp.int32) for x in xs])
    gates = (retain.T, step.T, momentum.T)

    def call(kernel, out, given, spaces=VMEM, scratch=(), outs=VMEM):
        return pl.pallas_call(
            kernel,
            out_shape=out,
            in_specs=[SMEM] + [spaces] * (len(given) - 1),
            out_specs=jax.tree.map(lambda _: outs, out),
            scratch_shapes=scratch,
            compiler_params=LIMIT,
        )(*given)

    turns = [*ORDER]

    def shift(piece, s, back=False):
        ends = (owners, teams) if back else (teams, owners)
        pairs = [(a[j], b[(j + s) % heads]) for a, b in zip(*ends) for j in range(heads)]
        return lax.ppermute(piece, axes, pairs)

    def behind(xs, y):
        return list(lax.optimization_barrier((*xs, y))[:-1])

    def make(shifts, given):
        given = [pltpu.with_memory_space_constraint(x, pltpu.HBM) for x in given]
        return call(
            functools.partial(map_kernel, heads, width, shifts),
            [shape(f32, 3 * width + TAIL, width)] * len(shifts),
            (scalars(mine), *given),
            HBM,
            [pltpu.VMEM(x.shape, x.dtype) for x in given] + [pltpu.SemaphoreType.DMA((len(given),))],
        )

    order = [*FIRSTS]
    made = dict(zip(order, make(order, (keys, values, *gates))))
    maps = [shift(made[s], s) for s in order]

    start = jnp.concatenate(
        [
            lax.dynamic_index_in_dim(init_memory, head, 0, keepdims=False),
            lax.dynamic_index_in_dim(init_moment, head, 0, keepdims=False),
        ],
        axis=1,
    )
    state = shape(f32, width, 2 * width)
    *unpacked, final = call(
        functools.partial(unpack_kernel, heads, width, order),
        [
            shape(bf16, heads, width, 2 * width),
            shape(bf16, heads, width, 2 * width),
            shape(f32, heads, 2 * width + TAIL, width),
            state,
        ],
        (scalars(head), start, *maps),
    )
    entry, other, flag = start, start, section < 0
    for s in range(sections - 1):
        if s > 0:
            entry, final = call(
                functools.partial(final_kernel, heads, width), [state] * 2, (scalars(flag), entry, other, *unpacked)
            )
        other = lax.ppermute(final, axes, list(zip(owners[s], owners[s + 1])))
        flag = section == s + 1
    states = call(
        functools.partial(states_kernel, heads, width),
        [state] * heads,
        (scalars(flag, head), entry, other, *unpacked),
        scratch=[pltpu.VMEM((heads, width, 2 * width), f32)],
    )
    pieces, moved = states, {}
    for n, s in enumerate(turns):
        if n == READ:
            given = behind((queries, keys, values, *gates), moved[turns[0]])
            reads = pl.pallas_call(
                functools.partial(read_kernel, heads, width),
                out_shape=[
                    shape(bf16, heads, length, 2 * width),
                    shape(bf16, heads, length, 2 * width),
                    shape(f32, heads, length, width),
                ],
                in_specs=[VMEM] * 6,
                out_specs=[VMEM] * 3,
                compiler_params=LIMIT,
            )(*given,)
        piece = pieces[s] if n < HELD else behind([pieces[s]], reads[2])[0]
        moved[s] = shift(piece, s, True)
    states = [moved[s] for s in range(heads)]
    early = call(
        functools.partial(early_kernel, heads),
        shape(bf16, EARLY, length, width),
        (scalars(mine), *reads, *states[:EARLY]),
    )
    return call(
        functools.partial(output_kernel, heads, width),
        shape(bf16, length, heads * width),
        (scalars(mine), *reads, early, *states[EARLY:]),
    )


def solution(mesh):
    rows = P(("groups", "outer", "inner"), None)
    return jax.shard_map(
        functools.partial(local, mesh.shape["outer"], mesh.shape["inner"]),
        mesh=mesh,
        in_specs=(rows,) * 6 + (P(), P()),
        out_specs=rows,
        check_vma=False,
    )
```

```python
import functools

import jax
import jax.numpy as jnp
from jax import lax
from jax.experimental import pallas as pl
from jax.experimental.pallas import tpu as pltpu
from jax.sharding import PartitionSpec as P

FIRSTS = (1, 2, 3, 4, 5, 6, 7, 0)
ORDER = (2, 4, 6, 3, 5, 0, 1, 7)
READ = 1
HELD = 8
EARLY = 5
TAIL = 8
EPS = 1e-06
EXACT = lax.Precision.HIGHEST


def halves(x):
    high = x.astype(jnp.bfloat16)
    return high, (x - high.astype(jnp.float32)).astype(jnp.bfloat16)


def mul(a, b, dims):
    return lax.dot_general(a, b, (dims, ((), ())), preferred_element_type=jnp.float32)


def mul_tn(a, b):
    return mul(a, b, ((0,), (0,)))


def mul_nt(a, b):
    return mul(a, b, ((1,), (1,)))


def mul_nn(a, b):
    return mul(a, b, ((1,), (0,)))


def exact(a, b):
    return jnp.dot(a, b, precision=EXACT, preferred_element_type=jnp.float32)


def grid_ids(shape):
    return lax.broadcasted_iota(jnp.int32, shape, 0), lax.broadcasted_iota(jnp.int32, shape, 1)


def lanes_of(h, width):
    return pl.ds(pl.multiple_of(h * width, width), width)


def map_kernel(heads, width, shifts, mine_ref, *refs):
    hbm, outs = refs[:5], refs[5 : 5 + len(shifts)]
    *held, sem = refs[5 + len(shifts) :]
    k_ref, v_ref, retain_ref, step_ref, momentum_ref = held
    copies = [pltpu.make_async_copy(s, t, sem.at[n]) for n, (s, t) in enumerate(zip(hbm, held))]
    for copy in copies[2:] + copies[:2]:
        copy.start()
    mine = mine_ref[0]
    length = k_ref.shape[0]
    row, col = grid_ids((length, length))
    before = (row <= col).astype(jnp.float32)
    after = (row >= col).astype(jnp.float32)
    drow, dcol = grid_ids((width, width))
    keep = drow <= dcol
    diagonal = drow == dcol
    for copy in copies[2:]:
        copy.wait()
    from_mine = lambda ref: pltpu.roll(ref[...], lax.rem(heads - mine, heads), 0)
    step = from_mine(step_ref)
    logs = exact(
        jnp.concatenate([jnp.log(from_mine(retain_ref)), jnp.log(from_mine(momentum_ref))], axis=0), before
    )
    log_retain, log_moment = logs[:heads], logs[heads:]
    decay = jnp.exp(log_moment)
    reach = jnp.exp(log_retain[:, length - 1 :] - log_retain) * decay
    suffix = exact(reach, after)
    memory_weight = (suffix / decay * step).T
    moment_weight = (jnp.exp(log_moment[:, length - 1 :] - log_moment) * step).T
    retain_end = jnp.exp(log_retain[:, length - 1 :])
    moment_end = decay[:, length - 1 :]
    carry_end = suffix[:, :1]
    for copy in copies[:2]:
        copy.wait()
    for n, s in enumerate(shifts):
        lanes = lanes_of(lax.rem(mine + s, heads), width)
        keys = k_ref[:, lanes]
        values = v_ref[:, lanes]
        wide = keys.astype(jnp.float32)
        scale = lax.rsqrt(jnp.sum(wide * wide, -1, keepdims=True) + EPS)
        weight_m = memory_weight[:, s : s + 1] * scale
        weight_s = moment_weight[:, s : s + 1] * scale
        write = jnp.concatenate([wide * weight_m, wide * weight_s], axis=1)
        high, low = halves(write)
        offset = mul_tn(values, high) + mul_tn(values, low)
        high, low = halves(write * scale)
        gram = mul_tn(keys, high) + mul_tn(keys, low)
        moment_gram = gram[:, width:]
        on_diagonal = jnp.sum(jnp.where(diagonal, moment_gram, 0.0), axis=0, keepdims=True)
        wide_row = lambda x: jnp.broadcast_to(x[s : s + 1, :], (1, width))
        out = outs[n]
        out[:width, :] = jnp.where(keep, gram[:, :width], moment_gram)
        out[width : 2 * width, :] = offset[:, :width]
        out[2 * width : 3 * width, :] = offset[:, width:]
        out[3 * width :, :] = jnp.concatenate(
            [
                on_diagonal,
                wide_row(retain_end),
                wide_row(moment_end),
                wide_row(carry_end),
                jnp.zeros((TAIL - 4, width), jnp.float32),
            ],
            axis=0,
        )


def read_kernel(
    heads, width, q_ref, k_ref, v_ref, retain_ref, step_ref, momentum_ref, high_ref, low_ref, base_ref
):
    length = k_ref.shape[0]
    row, col = grid_ids((length, length))
    before = (row <= col).astype(jnp.float32)
    causal = row >= col
    lower = causal.astype(jnp.bfloat16)
    logs = exact(jnp.concatenate([jnp.log(retain_ref[...]), jnp.log(momentum_ref[...])], axis=0), before)
    log_retain, log_moment = logs[:heads], logs[heads:]
    log_gap = log_moment - log_retain
    step_rows = step_ref[...] * jnp.exp(-log_moment)
    log_column = log_retain.T
    retain_scale = jnp.exp(log_column)
    ones = jnp.ones((8, width), jnp.bfloat16)
    for h in range(heads):
        lanes = slice(h * width, (h + 1) * width)
        queries, keys, values = q_ref[:, lanes], k_ref[:, lanes], v_ref[:, lanes]
        wide_q = queries.astype(jnp.float32)
        wide_k = keys.astype(jnp.float32)
        query_scale = lax.rsqrt(jnp.sum(wide_q * wide_q, -1, keepdims=True) + EPS)
        high, low = halves(wide_k * wide_k)
        key_scale = lax.rsqrt((mul_nt(ones, high) + mul_nt(ones, low))[:1, :] + EPS)
        gap = log_column[:, h : h + 1] + log_gap[h : h + 1, :]
        reach = jnp.exp(jnp.where(causal, gap, -1e30))
        high, low = halves(reach)
        weights = mul_nn(high, lower) + mul_nn(low, lower)
        mixing = mul_nt(queries, keys) * weights * (step_rows[h : h + 1, :] * key_scale)
        high, low = halves(mixing)
        base_ref[h] = query_scale * (mul_nn(high, values) + mul_nn(low, values))
        high, low = halves(mixing * key_scale)
        seen = mul_nn(high, keys) + mul_nn(low, keys)
        unit_q = query_scale * wide_q
        reads = jnp.concatenate(
            [retain_scale[:, h : h + 1] * unit_q - query_scale * seen, weights[:, :1] * unit_q], axis=1
        )
        high, low = halves(reads)
        high_ref[h] = high
        low_ref[h] = low


def steps(width, state, high_ref, low_ref, offset_ref, count, keep=None):
    for b in range(count):
        if keep is not None:
            keep[b] = state
        tail = offset_ref[b, 2 * width :, :]
        memory, moment = state[:, :width], state[:, width:]
        high, low = halves(memory)
        seen = mul_nn(high, high_ref[b]) + (mul_nn(high, low_ref[b]) + mul_nn(low, high_ref[b]))
        new_memory = tail[1:2, :] * memory + tail[3:4, :] * moment + offset_ref[b, :width, :] - seen[:, :width]
        new_moment = tail[2:3, :] * moment + offset_ref[b, width : 2 * width, :] - seen[:, width:]
        state = jnp.concatenate([new_memory, new_moment], axis=1)
    return state


def unpack_kernel(heads, width, order, mine_ref, entry_ref, *refs):
    arrived, (high_ref, low_ref, offset_ref, final_ref) = refs[:heads], refs[heads:]
    mine = mine_ref[0]
    row, col = grid_ids((width, width))
    for n, s in enumerate(order):
        b = lax.rem(mine + heads - s, heads)
        packed = arrived[n][:width, :]
        flipped = packed.T
        diagonal = arrived[n][3 * width : 3 * width + 1, :]
        gram = jnp.concatenate(
            [
                jnp.where(row <= col, packed, flipped),
                jnp.where(row == col, diagonal, jnp.where(row > col, packed, flipped)),
            ],
            axis=1,
        )
        high, low = halves(gram)
        high_ref[b] = high
        low_ref[b] = low
        offset_ref[b] = arrived[n][width:, :]
    final_ref[...] = steps(width, entry_ref[...], high_ref, low_ref, offset_ref, heads)


def final_kernel(heads, width, flag_ref, entry_ref, other_ref, high_ref, low_ref, offset_ref, kept_ref, final_ref):
    entry = jnp.where(flag_ref[0] > 0, other_ref[...], entry_ref[...])
    kept_ref[...] = entry
    final_ref[...] = steps(width, entry, high_ref, low_ref, offset_ref, heads)


def states_kernel(heads, width, scalar_ref, entry_ref, other_ref, high_ref, low_ref, offset_ref, *refs):
    outs, keep = refs[:heads], refs[heads]
    mine = scalar_ref[1]
    entry = jnp.where(scalar_ref[0] > 0, other_ref[...], entry_ref[...])
    keep[heads - 1] = steps(width, entry, high_ref, low_ref, offset_ref, heads - 1, keep)
    for s in range(heads):
        outs[s][...] = keep[lax.rem(mine + s, heads)]


def read_out(h, state, read_high_ref, read_low_ref, base_ref):
    high, low = halves(state)
    read_high = read_high_ref[h]
    result = base_ref[h] + mul_nt(read_high, high)
    return (result + (mul_nt(read_high, low) + mul_nt(read_low_ref[h], high))).astype(jnp.bfloat16)


def early_kernel(heads, mine_ref, read_high_ref, read_low_ref, base_ref, *refs):
    *arrived, out_ref = refs
    mine = mine_ref[0]
    for s, ref in enumerate(arrived):
        h = lax.rem(mine + heads - s, heads)
        out_ref[s] = read_out(h, ref[...], read_high_ref, read_low_ref, base_ref)


def output_kernel(heads, width, mine_ref, read_high_ref, read_low_ref, base_ref, early_ref, *refs):
    *arrived, out_ref = refs
    mine = mine_ref[0]
    early = heads - len(arrived)
    for s in range(heads):
        h = lax.rem(mine + heads - s, heads)
        if s < early:
            result = early_ref[s]
        else:
            result = read_out(h, arrived[s - early][...], read_high_ref, read_low_ref, base_ref)
        out_ref[:, lanes_of(h, width)] = result


VMEM = pl.BlockSpec(memory_space=pltpu.VMEM)
HBM = pl.BlockSpec(memory_space=pltpu.HBM)
SMEM = pl.BlockSpec(memory_space=pltpu.SMEM)
LIMIT = pltpu.CompilerParams(vmem_limit_bytes=24 << 20)


def shape(kind, *sizes):
    return jax.ShapeDtypeStruct(sizes, kind)


def local(n_outer, n_inner, queries, keys, values, retain, step, momentum, init_memory, init_moment):
    length, heads = retain.shape
    width = init_memory.shape[2]
    f32, bf16 = jnp.float32, jnp.bfloat16
    axes = ("inner", "outer")
    place = lambda f: (f % n_inner) * n_outer + f // n_inner
    sections = n_outer * n_inner // heads
    teams = [[place(s * heads + j) for j in range(heads)] for s in range(sections)]
    position = lax.axis_index("outer") * n_inner + lax.axis_index("inner")
    mine = position % heads
    if heads % n_inner == 0 and n_outer == sections * (heads // n_inner):
        owners = [
            [place((h // n_inner * sections + s) * n_inner + h % n_inner) for h in range(heads)]
            for s in range(sections)
        ]
        outer = lax.axis_index("outer")
        section, head = outer % sections, outer // sections * n_inner + lax.axis_index("inner")
    else:
        owners, section, head = teams, position // heads, mine
    scalars = lambda *xs: jnp.stack([jnp.asarray(x).astype(jnp.int32) for x in xs])
    gates = (retain.T, step.T, momentum.T)

    def call(kernel, out, given, spaces=VMEM, scratch=(), outs=VMEM):
        return pl.pallas_call(
            kernel,
            out_shape=out,
            in_specs=[SMEM] + [spaces] * (len(given) - 1),
            out_specs=jax.tree.map(lambda _: outs, out),
            scratch_shapes=scratch,
            compiler_params=LIMIT,
        )(*given)

    turns = [*ORDER]

    def shift(piece, s, back=False):
        ends = (owners, teams) if back else (teams, owners)
        pairs = [(a[j], b[(j + s) % heads]) for a, b in zip(*ends) for j in range(heads)]
        return lax.ppermute(piece, axes, pairs)

    def behind(xs, y):
        return list(lax.optimization_barrier((*xs, y))[:-1])

    def make(shifts, given):
        given = [pltpu.with_memory_space_constraint(x, pltpu.HBM) for x in given]
        return call(
            functools.partial(map_kernel, heads, width, shifts),
            [shape(f32, 3 * width + TAIL, width)] * len(shifts),
            (scalars(mine), *given),
            HBM,
            [pltpu.VMEM(x.shape, x.dtype) for x in given] + [pltpu.SemaphoreType.DMA((len(given),))],
        )

    order = [*FIRSTS]
    made = dict(zip(order, make(order, (keys, values, *gates))))
    maps = [shift(made[s], s) for s in order]

    start = jnp.concatenate(
        [
            lax.dynamic_index_in_dim(init_memory, head, 0, keepdims=False),
            lax.dynamic_index_in_dim(init_moment, head, 0, keepdims=False),
        ],
        axis=1,
    )
    state = shape(f32, width, 2 * width)
    *unpacked, final = call(
        functools.partial(unpack_kernel, heads, width, order),
        [
            shape(bf16, heads, width, 2 * width),
            shape(bf16, heads, width, 2 * width),
            shape(f32, heads, 2 * width + TAIL, width),
            state,
        ],
        (scalars(head), start, *maps),
    )
    entry, other, flag = start, start, section < 0
    for s in range(sections - 1):
        if s > 0:
            entry, final = call(
                functools.partial(final_kernel, heads, width), [state] * 2, (scalars(flag), entry, other, *unpacked)
            )
        other = lax.ppermute(final, axes, list(zip(owners[s], owners[s + 1])))
        flag = section == s + 1
    states = call(
        functools.partial(states_kernel, heads, width),
        [state] * heads,
        (scalars(flag, head), entry, other, *unpacked),
        scratch=[pltpu.VMEM((heads, width, 2 * width), f32)],
    )
    pieces, moved = states, {}
    for n, s in enumerate(turns):
        if n == READ:
            given = behind((queries, keys, values, *gates), moved[turns[0]])
            reads = pl.pallas_call(
                functools.partial(read_kernel, heads, width),
                out_shape=[
                    shape(bf16, heads, length, 2 * width),
                    shape(bf16, heads, length, 2 * width),
                    shape(f32, heads, length, width),
                ],
                in_specs=[VMEM] * 6,
                out_specs=[VMEM] * 3,
                compiler_params=LIMIT,
            )(*given,)
        piece = pieces[s] if n < HELD else behind([pieces[s]], reads[2])[0]
        moved[s] = shift(piece, s, True)
    states = [moved[s] for s in range(heads)]
    early = call(
        functools.partial(early_kernel, heads),
        shape(bf16, EARLY, length, width),
        (scalars(mine), *reads, *states[:EARLY]),
    )
    return call(
        functools.partial(output_kernel, heads, width),
        shape(bf16, length, heads * width),
        (scalars(mine), *reads, early, *states[EARLY:]),
    )


def solution(mesh):
    rows = P(("groups", "outer", "inner"), None)
    return jax.shard_map(
        functools.partial(local, mesh.shape["outer"], mesh.shape["inner"]),
        mesh=mesh,
        in_specs=(rows,) * 6 + (P(), P()),
        out_specs=rows,
        check_vma=False,
    )
```
